1024 devices in a mesh: row: 32 (over x, z_lo), col: 32 (over z_hi, y, core).
Axes of the slice: x: 8, y: 8, z: 8 (z_hi: 2, z_lo: 4; z = z_hi * 4 + z_lo), core: 2. Of those that a mesh axis runs over, the one named last changes fastest.
Arguments:
- estimate: float32 [8, 1024, 4096], P(None, 'row', 'col'), may hold values from 0.5 to 2
- views_data: bfloat16 [4, 8, 1024, 4096], P(None, None, 'row', 'col'), may hold values from 0.25 to 4
- psf_rows: float32 [4, 33], replicated, may hold values from 0.05 to 1
- psf_cols: float32 [4, 33], replicated, may hold values from 0.05 to 1
Outputs:
- estimate_next: float32 [8, 1024, 4096], P(None, 'row', 'col')
The draws below stay inside these ranges and needn't reach their ends.
All inputs are finite; a program needn't handle non-finite values.
Results may differ from the reference program's by a relative error of at most 0.0003.
Values may be sent and summed in bfloat16 or wider, within the bound.
No kernel may reach another device: no remote copies, remote signals or barrier semaphores. Data moves between devices by JAX's collectives and lax.ppermute only.
A program may use at most 32 MiB of HBM per device.

```python
import math
import jax
import jax.numpy as jnp
from jax import lax

VIEWS = 4
KW = 33
PLANES = 8
NY = 1024
NX = 4096


def level_of(stream_key, shape, split, least, high):
    level, own = 1.0, jax.random.fold_in(stream_key, 6)
    for position, parts in split:
        draws = jnp.exp(jax.random.uniform(jax.random.fold_in(own, position), (parts,), jnp.float32, least / len(split), high / len(split)))
        level = level * jnp.repeat(draws, shape[position] // parts).reshape([-1 if axis == position else 1 for axis in range(len(shape))])
    return level


def setup_inputs(seed: int = 0) -> dict:
    arg_keys = jax.random.split(jax.random.key(seed), 5)
    estimate = jnp.clip(0.5 + 1.5 * jax.random.uniform(arg_keys[0], (PLANES, NY, NX), jnp.float32) ** level_of(arg_keys[0], (PLANES, NY, NX), ((1, 32), (2, 32)), -0.2, 0.2), 0.5, 2.0)
    views_data = jnp.clip(jnp.exp(math.log(4.0) - 2.7725887 * jax.random.uniform(arg_keys[1], (VIEWS, PLANES, NY, NX), jnp.float32) ** level_of(arg_keys[1], (VIEWS, PLANES, NY, NX), ((2, 32), (3, 32)), -0.2, 0.2)), 0.25, 4.0).astype(jnp.bfloat16)
    psf_rows = jnp.clip(jnp.exp(jax.random.uniform(arg_keys[2], (VIEWS, KW), jnp.float32, math.log(0.05), math.log(1.0))), 0.05, 1.0)
    psf_cols = jnp.clip(jnp.exp(jax.random.uniform(arg_keys[3], (VIEWS, KW), jnp.float32, math.log(0.05), math.log(1.0))), 0.05, 1.0)
    return dict(estimate=estimate, views_data=views_data, psf_rows=psf_rows, psf_cols=psf_cols)


def blur_along(source, kernel, along_axis):
    reach = (kernel.shape[0] - 1) // 2
    lhs = source[:, None, :, :]
    if along_axis == 0:
        rhs = kernel.reshape(1, 1, kernel.shape[0], 1)
        padding = ((reach, reach), (0, 0))
    else:
        rhs = kernel.reshape(1, 1, 1, kernel.shape[0])
        padding = ((0, 0), (reach, reach))
    result = lax.conv_general_dilated(lhs, rhs, (1, 1), padding, precision=lax.Precision.HIGHEST)
    return result[:, 0, :, :]


def reference(estimate, views_data, psf_rows, psf_cols):
    kernels_y = psf_rows / jnp.sum(psf_rows, axis=1, keepdims=True)
    kernels_x = psf_cols / jnp.sum(psf_cols, axis=1, keepdims=True)
    log_sum = jnp.zeros(estimate.shape, jnp.float32)
    for view_index in range(VIEWS):
        blurred = blur_along(blur_along(estimate, kernels_x[view_index], 1), kernels_y[view_index], 0)
        quotient = views_data[view_index].astype(jnp.float32) / blurred
        correction = blur_along(blur_along(quotient, kernels_x[view_index][::-1], 1), kernels_y[view_index][::-1], 0)
        log_sum = log_sum + jnp.log(correction)
    return estimate * jnp.exp(log_sum / VIEWS)
```

```python
import functools

import jax
import jax.numpy as jnp
from jax import lax
from jax.experimental import pallas as pl
from jax.experimental.pallas import tpu as pltpu
from jax.sharding import PartitionSpec as P

F32, BF16 = jnp.float32, jnp.bfloat16
LANES = 128
WIDE = 2 * LANES


def iota(shape, dim):
    return lax.broadcasted_iota(jnp.int32, shape, dim)


def pack_kernel(dims, est_ref, views_ref, first_ref, second_ref):
    views, planes, rows, reach = dims
    odd = lax.rem(lax.axis_index("col"), 2) == 1
    wide, group = 2 * reach, LANES // (2 * reach)
    lane = iota((rows, LANES), 1)

    def strips(load, width, count):
        low = high = jnp.zeros((rows, LANES), F32)
        for k in range(count):
            block = load(k)
            here = (lane >= k * width) & (lane < (k + 1) * width)
            low = jnp.where(here, pltpu.roll(block, k * width, 1), low)
            high = jnp.where(here, pltpu.roll(block, (k + 1) * width % LANES, 1), high)
        return low, high

    def put(at, low, high):
        low, high = low.astype(BF16), high.astype(BF16)
        first_ref[at : at + rows, :] = jnp.where(odd, low, high)
        second_ref[at : at + rows, :] = jnp.where(odd, high, low)

    for t in range(planes // group):
        put(t * rows, *strips(lambda k: est_ref[t * group + k], wide, group))
    base = planes // group * rows
    for v in range(views):
        put(base + v * rows, *strips(lambda k: views_ref[v, k].astype(F32), reach, planes))


def rows_kernel(dims, est_ref, views_ref, first_ref, second_ref):
    views, planes, rows, reach = dims
    odd = lax.rem(lax.axis_index("row"), 2) == 1
    for p in range(planes):
        own = est_ref[p].astype(BF16)
        for ref in (first_ref, second_ref):
            ref[p * rows : (p + 1) * rows, :] = own
    at = planes * rows
    for v in range(views):
        for p in range(planes):
            top, bottom = views_ref[v, p, 0:reach, :], views_ref[v, p, rows - reach : rows, :]
            first_ref[at : at + reach, :] = jnp.where(odd, top, bottom)
            second_ref[at : at + reach, :] = jnp.where(odd, bottom, top)
            at += reach


def corners_kernel(dims, _1, _2, c1_ref, c2_ref, first_ref, second_ref):
    views, planes, rows, reach = dims
    odd = lax.rem(lax.axis_index("row"), 2) == 1
    strip = planes * 2 * reach // LANES * rows
    at = planes * rows + views * planes * reach
    for c in (c1_ref, c2_ref):
        for ref in (first_ref, second_ref):
            ref[at : at + strip, :] = c[0:strip, :]
        at += strip
    for c in (c1_ref, c2_ref):
        for v in range(views):
            base = strip + v * rows
            top, bottom = c[base : base + reach, :], c[base + rows - reach : base + rows, :]
            first_ref[at : at + reach, :] = jnp.where(odd, top, bottom)
            second_ref[at : at + reach, :] = jnp.where(odd, bottom, top)
            at += reach


def bands_kernel(dims, psf_y_ref, psf_x_ref, ky_ref, kx_ref, kxt_ref, kyt_ref, taps_ref):
    views, planes, rows, reach = dims
    taps = 2 * reach + 1
    tall, full = rows + 2 * reach, rows + 4 * reach
    taps_ref[...] = jnp.zeros(taps_ref.shape, F32)
    for i, ref in enumerate((psf_y_ref, psf_x_ref)):
        psf = ref[...]
        taps_ref[i, 0:views, 0:taps] = psf / jnp.sum(psf, axis=1, keepdims=True)

    def band(i, v, tap, valid):
        source = jnp.broadcast_to(taps_ref[i, v : v + 1, :], tap.shape)
        inside = valid & (tap >= 0) & (tap < taps)
        return jnp.take_along_axis(source, jnp.where(inside, tap, LANES - 1), axis=1)

    def halves(w):
        hi = w.astype(BF16)
        return hi, (w - hi.astype(F32)).astype(BF16)

    def column(j, width):
        x = jnp.where(j < LANES, j, jnp.where(j < LANES + width, j - LANES - width, j - width))
        return x, j < LANES + 2 * width

    for half in range(2):
        lanes = slice(half * LANES, (half + 1) * LANES)
        row, lane = iota((tall, LANES), 0), iota((tall, LANES), 1) + half * LANES
        for v in range(views):
            hi, lo = halves(band(0, v, lax.rem(lane, full) - row, lane < 2 * full))
            ky_ref[v * tall : (v + 1) * tall, lanes] = jnp.where(lane < full, hi.astype(F32), lo.astype(F32)).astype(BF16)
        row, lane = iota((rows, LANES), 0), iota((rows, LANES), 1) + half * LANES
        for v in range(views):
            hi, lo = halves(band(0, v, row - lax.rem(lane, tall) + 2 * reach, lane < 3 * tall))
            pick = (lane >= tall) & (lane < 2 * tall)
            kyt_ref[v * rows : (v + 1) * rows, lanes] = jnp.where(pick, lo.astype(F32), hi.astype(F32)).astype(BF16)
        shape = (WIDE, LANES)
        source, ok_source = column(iota(shape, 0), 2 * reach)
        target, ok_target = column(iota(shape, 1) + half * LANES, reach)
        tap, ok = source - target + reach, ok_source & ok_target
        for v in range(views):
            kx_ref[v, :, lanes] = band(1, v, tap, ok).astype(BF16)
    source, ok = column(iota(shape, 0), reach)
    tap = iota(shape, 1) - source + reach
    for v in range(views):
        kxt_ref[v] = band(1, v, tap, ok).astype(BF16)


def step_kernel(dims, est_ref, views_ref, c1_ref, c2_ref, r1_ref, r2_ref, ky_ref, kx_ref, kxt_ref, kyt_ref, out_ref):
    views, planes, rows, reach = dims
    wide, group = 2 * reach, LANES // (2 * reach)
    tall = rows + 2 * reach
    tiles = planes // group
    odd_col = lax.rem(lax.axis_index("col"), 2) == 1
    odd_row = lax.rem(lax.axis_index("row"), 2) == 1

    def pair(odd, one, two):
        return jnp.where(odd, one, two), jnp.where(odd, two, one)

    own = planes * rows
    at_views = own
    at_c = own + views * planes * reach
    at_cv = at_c + 2 * tiles * rows

    def edge(at, n):
        return pair(odd_row, r1_ref[at : at + n, :], r2_ref[at : at + n, :])

    blocks = []
    lane = iota((rows + 4 * reach, LANES), 1)
    halo = []
    for t in range(tiles):
        above1, below1 = edge(at_c + t * rows, rows)
        above2, below2 = edge(at_c + (tiles + t) * rows, rows)
        own1, own2 = c1_ref[t * rows : (t + 1) * rows, :], c2_ref[t * rows : (t + 1) * rows, :]
        one = jnp.concatenate([above1, own1, below1], axis=0).astype(F32)
        two = jnp.concatenate([above2, own2, below2], axis=0).astype(F32)
        halo.append(pair(odd_col, one, two))
    for p in range(planes):
        above, below = edge(p * rows, rows)
        blocks.append(jnp.concatenate([above, est_ref[p].astype(BF16), below], axis=0))
        left, right = halo[p // group]
        k = p % group
        left = pltpu.roll(left, (LANES - k * wide) % LANES, 1)
        right = pltpu.roll(right, (LANES + wide - k * wide) % LANES, 1)
        blocks.append(jnp.where(lane < wide, left, right).astype(BF16))
    field = jnp.concatenate(blocks, axis=1)
    field = jnp.concatenate([field, field, jnp.zeros((WIDE - 2 * field.shape[0], field.shape[1]), BF16)], axis=0)

    lane = iota((tall, LANES), 1)
    product = None
    every = [
        jnp.dot(ky_ref[...], field[:, p * WIDE : (p + 1) * WIDE], preferred_element_type=F32).astype(BF16)
        for p in range(planes)
    ]
    for v in range(views):
        rowed = jnp.concatenate([every[p][v * tall : (v + 1) * tall, :] for p in range(planes)], axis=0)
        blurred = jnp.dot(rowed, kx_ref[v], preferred_element_type=F32)
        above1, below1 = edge(at_cv + v * reach, reach)
        above2, below2 = edge(at_cv + (views + v) * reach, reach)
        base = tiles * rows + v * rows
        one = jnp.concatenate([above1, c1_ref[base : base + rows, :], below1], axis=0).astype(F32)
        two = jnp.concatenate([above2, c2_ref[base : base + rows, :], below2], axis=0).astype(F32)
        left, right = pair(odd_col, one, two)
        quotients = []
        for p in range(planes):
            above, below = edge(at_views + (v * planes + p) * reach, reach)
            data = jnp.concatenate([above, views_ref[v, p], below], axis=0).astype(F32)
            here = blurred[p * tall : (p + 1) * tall, :]
            main = data / here[:, :LANES]
            l = pltpu.roll(left, (LANES - p * reach) % LANES, 1)
            r = pltpu.roll(right, (LANES + reach - p * reach) % LANES, 1)
            rim = jnp.where(lane < reach, l, r) / jnp.where(lane < wide, here[:, LANES:], 1.0)
            rim = jnp.where(lane < wide, rim, 0.0)
            quotients.append(jnp.concatenate([main.astype(BF16), rim.astype(BF16)], axis=1))
        quotient = jnp.concatenate(quotients, axis=0)
        back = jnp.dot(quotient, kxt_ref[v], preferred_element_type=F32)
        hi = back.astype(BF16)
        lo = (back - hi.astype(F32)).astype(BF16)

        def planes_along_lanes(a):
            return jnp.concatenate([a[p * tall : (p + 1) * tall, :] for p in range(planes)], axis=1)

        hi, lo = planes_along_lanes(hi), planes_along_lanes(lo)
        back = jnp.concatenate([hi, hi, lo, jnp.zeros((WIDE - 3 * tall, planes * LANES), BF16)], axis=0)
        correction = jnp.dot(kyt_ref[v * rows : (v + 1) * rows, :], back, preferred_element_type=F32)
        product = correction if product is None else product * correction
    factor = jnp.sqrt(jnp.sqrt(product))
    for p in range(planes):
        out_ref[p] = est_ref[p] * factor[:, p * LANES : (p + 1) * LANES]


def swaps(size, start):
    return [pair for i in range(start, size - 1, 2) for pair in ((i, i + 1), (i + 1, i))]


def local(estimate, views_data, psf_rows, psf_cols):
    views, planes, rows, _ = views_data.shape
    reach = (psf_rows.shape[1] - 1) // 2
    dims = (views, planes, rows, reach)
    tiles = planes * 2 * reach // LANES
    strip = (tiles + views) * rows
    vmem = pl.BlockSpec(memory_space=pltpu.VMEM)
    params = pltpu.CompilerParams(vmem_limit_bytes=16 << 20)

    def call(kernel, n_in, outs, scratch=(), aliases={}):
        return pl.pallas_call(
            functools.partial(kernel, dims),
            out_shape=outs,
            in_specs=[vmem] * n_in,
            out_specs=jax.tree.map(lambda _: vmem, outs),
            scratch_shapes=scratch,
            input_output_aliases=aliases,
            compiler_params=params,
            cost_estimate=pl.CostEstimate(flops=1 << 20, bytes_accessed=1 << 20, transcendentals=0),
        )

    message = jax.ShapeDtypeStruct((strip, LANES), BF16)
    first, second = call(pack_kernel, 2, (message, message))(estimate, views_data)
    size = lax.axis_size("col")
    c1 = lax.ppermute(first, "col", swaps(size, 0))
    c2 = lax.ppermute(second, "col", swaps(size, 1))

    tall = rows + 2 * reach
    bands = call(
        bands_kernel,
        2,
        (
            jax.ShapeDtypeStruct((views * tall, WIDE), BF16),
            jax.ShapeDtypeStruct((views, WIDE, WIDE), BF16),
            jax.ShapeDtypeStruct((views, WIDE, LANES), BF16),
            jax.ShapeDtypeStruct((views * rows, WIDE), BF16),
        ),
        [pltpu.VMEM((2, 8, LANES), F32)],
    )(psf_rows, psf_cols)

    length = planes * rows + views * planes * reach + 2 * (tiles * rows + views * reach)
    message = jax.ShapeDtypeStruct((length, LANES), BF16)
    first, second = call(rows_kernel, 2, (message, message))(estimate, views_data)
    first, second = call(corners_kernel, 4, (message, message), aliases={0: 0, 1: 1})(first, second, c1, c2)
    size = lax.axis_size("row")
    r1 = lax.ppermute(first, "row", swaps(size, 0))
    r2 = lax.ppermute(second, "row", swaps(size, 1))
    return call(step_kernel, 10, jax.ShapeDtypeStruct(estimate.shape, F32))(
        estimate, views_data, c1, c2, r1, r2, *bands
    )


def solution(mesh):
    return jax.shard_map(
        local,
        mesh=mesh,
        in_specs=(P(None, "row", "col"), P(None, None, "row", "col"), P(), P()),
        out_specs=P(None, "row", "col"),
        check_vma=False,
    )
```

```python
import functools

import jax
import jax.numpy as jnp
from jax import lax
from jax.experimental import pallas as pl
from jax.experimental.pallas import tpu as pltpu
from jax.sharding import PartitionSpec as P

F32, BF16 = jnp.float32, jnp.bfloat16
LANES = 128
WIDE = 2 * LANES


def iota(shape, dim):
    return lax.broadcasted_iota(jnp.int32, shape, dim)


def pack_kernel(dims, est_hbm, views_hbm, low_ref, high_ref, est_ref, views_ref, sems):
    views, planes, rows, reach = dims
    wide, group = 2 * reach, LANES // (2 * reach)
    lane = iota((rows, LANES), 1)
    copies = [
        pltpu.make_async_copy(hbm, ref, sems.at[i])
        for i, (hbm, ref) in enumerate(((est_hbm, est_ref), (views_hbm, views_ref)))
    ]
    for copy in copies:
        copy.start()

    def strips(at, load, width, count):
        low = high = jnp.zeros((rows, LANES), F32)
        for k in range(count):
            block = load(k)
            here = (lane >= k * width) & (lane < (k + 1) * width)
            low = jnp.where(here, pltpu.roll(block, k * width, 1), low)
            high = jnp.where(here, pltpu.roll(block, (k + 1) * width % LANES, 1), high)
        low_ref[at : at + rows, :] = low.astype(BF16)
        high_ref[at : at + rows, :] = high.astype(BF16)

    copies[0].wait()
    for t in range(planes // group):
        strips(t * rows, lambda k: est_ref[t * group + k], wide, group)
    base = planes // group * rows
    copies[1].wait()
    for v in range(views):
        strips(base + v * rows, lambda k: views_ref[v, k].astype(F32), reach, planes)


def rows_kernel(dims, est_ref, views_ref, right_ref, left_ref, bottom_ref, top_ref):
    views, planes, rows, reach = dims
    strip = planes * 2 * reach // LANES * rows
    at = 0

    def both(block):
        for ref in (bottom_ref, top_ref):
            ref[at : at + block.shape[0], :] = block
        return at + block.shape[0]

    def sides(ref, base):
        top_ref[at : at + reach, :] = ref[base : base + reach, :]
        bottom_ref[at : at + reach, :] = ref[base + rows - reach : base + rows, :]
        return at + reach

    for p in range(planes):
        at = both(est_ref[p].astype(BF16))
    for v in range(views):
        for p in range(planes):
            at = sides(views_ref.at[v, p], 0)
    for c in (left_ref, right_ref):
        at = both(c[0:strip, :])
    for c in (left_ref, right_ref):
        for v in range(views):
            at = sides(c, strip + v * rows)


def bands_kernel(dims, psf_y_ref, psf_x_ref, ky_ref, kx_ref, kxt_ref, kyt_ref, taps_ref):
    views, planes, rows, reach = dims
    taps = 2 * reach + 1
    tall, full = rows + 2 * reach, rows + 4 * reach
    taps_ref[...] = jnp.zeros(taps_ref.shape, F32)
    for i, ref in enumerate((psf_y_ref, psf_x_ref)):
        psf = ref[...]
        taps_ref[i, 0:views, 0:taps] = psf / jnp.sum(psf, axis=1, keepdims=True)

    def band(i, v, tap, valid):
        source = jnp.broadcast_to(taps_ref[i, v : v + 1, :], tap.shape)
        inside = valid & (tap >= 0) & (tap < taps)
        return jnp.take_along_axis(source, jnp.where(inside, tap, LANES - 1), axis=1)

    def halves(w):
        hi = w.astype(BF16)
        return hi, (w - hi.astype(F32)).astype(BF16)

    def column(j, width):
        x = jnp.where(j < LANES, j, jnp.where(j < LANES + width, j - LANES - width, j - width))
        return x, j < LANES + 2 * width

    for half in range(2):
        lanes = slice(half * LANES, (half + 1) * LANES)
        row, lane = iota((tall, LANES), 0), iota((tall, LANES), 1) + half * LANES
        for v in range(views):
            hi, lo = halves(band(0, v, lax.rem(lane, full) - row, lane < 2 * full))
            ky_ref[v * tall : (v + 1) * tall, lanes] = jnp.where(lane < full, hi.astype(F32), lo.astype(F32)).astype(BF16)
        row, lane = iota((rows, LANES), 0), iota((rows, LANES), 1) + half * LANES
        for v in range(views):
            hi, lo = halves(band(0, v, row - lax.rem(lane, tall) + 2 * reach, lane < 3 * tall))
            pick = (lane >= tall) & (lane < 2 * tall)
            kyt_ref[v * rows : (v + 1) * rows, lanes] = jnp.where(pick, lo.astype(F32), hi.astype(F32)).astype(BF16)
        shape = (WIDE, LANES)
        source, ok_source = column(iota(shape, 0), 2 * reach)
        target, ok_target = column(iota(shape, 1) + half * LANES, reach)
        tap, ok = source - target + reach, ok_source & ok_target
        for v in range(views):
            kx_ref[v, :, lanes] = band(1, v, tap, ok).astype(BF16)
    source, ok = column(iota(shape, 0), reach)
    tap = iota(shape, 1) - source + reach
    for v in range(views):
        kxt_ref[v] = band(1, v, tap, ok).astype(BF16)


def step_kernel(dims, est_ref, views_ref, right_ref, left_ref, above_ref, below_ref, ky_ref, kx_ref, kxt_ref, kyt_ref, out_ref):
    views, planes, rows, reach = dims
    wide, group = 2 * reach, LANES // (2 * reach)
    tall = rows + 2 * reach
    tiles = planes // group
    own = planes * rows
    at_views = own
    at_c = own + views * planes * reach
    at_cv = at_c + 2 * tiles * rows

    def tower(at, n, own):
        return jnp.concatenate([above_ref[at : at + n, :], own, below_ref[at : at + n, :]], axis=0)

    blocks = []
    lane = iota((rows + 4 * reach, LANES), 1)
    halo = []
    for t in range(tiles):
        own = slice(t * rows, (t + 1) * rows)
        left = tower(at_c + t * rows, rows, left_ref[own, :]).astype(F32)
        right = tower(at_c + (tiles + t) * rows, rows, right_ref[own, :]).astype(F32)
        halo.append((left, right))
    for p in range(planes):
        blocks.append(tower(p * rows, rows, est_ref[p].astype(BF16)))
        left, right = halo[p // group]
        k = p % group
        left = pltpu.roll(left, (LANES - k * wide) % LANES, 1)
        right = pltpu.roll(right, (LANES + wide - k * wide) % LANES, 1)
        blocks.append(jnp.where(lane < wide, left, right).astype(BF16))
    field = jnp.concatenate(blocks, axis=1)
    field = jnp.concatenate([field, field, jnp.zeros((WIDE - 2 * field.shape[0], field.shape[1]), BF16)], axis=0)

    lane = iota((tall, LANES), 1)
    product = None
    every = [
        jnp.dot(ky_ref[...], field[:, p * WIDE : (p + 1) * WIDE], preferred_element_type=F32).astype(BF16)
        for p in range(planes)
    ]
    def blur(v):
        rowed = jnp.concatenate([every[p][v * tall : (v + 1) * tall, :] for p in range(planes)], axis=0)
        return jnp.dot(rowed, kx_ref[v], preferred_element_type=F32)

    def divide(v, blurred):
        own = slice((tiles + v) * rows, (tiles + v + 1) * rows)
        left = tower(at_cv + v * reach, reach, left_ref[own, :]).astype(F32)
        right = tower(at_cv + (views + v) * reach, reach, right_ref[own, :]).astype(F32)
        quotients = []
        for p in range(planes):
            data = tower(at_views + (v * planes + p) * reach, reach, views_ref[v, p]).astype(F32)
            here = blurred[p * tall : (p + 1) * tall, :]
            main = data / here[:, :LANES]
            l = pltpu.roll(left, (LANES - p * reach) % LANES, 1)
            r = pltpu.roll(right, (LANES + reach - p * reach) % LANES, 1)
            rim = jnp.where(lane < reach, l, r) / jnp.where(lane < wide, here[:, LANES:], 1.0)
            rim = jnp.where(lane < wide, rim, 0.0)
            quotients.append(jnp.concatenate([main.astype(BF16), rim.astype(BF16)], axis=1))
        return jnp.concatenate(quotients, axis=0)

    def planes_along_lanes(a):
        return jnp.concatenate([a[p * tall : (p + 1) * tall, :] for p in range(planes)], axis=1)

    def blur_back(v, quotient):
        back = jnp.dot(quotient, kxt_ref[v], preferred_element_type=F32)
        hi = back.astype(BF16)
        lo = (back - hi.astype(F32)).astype(BF16)
        hi, lo = planes_along_lanes(hi), planes_along_lanes(lo)
        return jnp.concatenate([hi, hi, lo, jnp.zeros((WIDE - 3 * tall, planes * LANES), BF16)], axis=0)

    def correct(v, back):
        return jnp.dot(kyt_ref[v * rows : (v + 1) * rows, :], back, preferred_element_type=F32)

    blurred = [blur(v) for v in range(views)]
    quotient = [divide(v, b) for v, b in enumerate(blurred)]
    back = [blur_back(v, q) for v, q in enumerate(quotient)]
    product = functools.reduce(jnp.multiply, [correct(v, b) for v, b in enumerate(back)])
    factor = jnp.sqrt(jnp.sqrt(product))
    for p in range(planes):
        out_ref[p] = est_ref[p] * factor[:, p * LANES : (p + 1) * LANES]


def shift(array, axis, step):
    size = lax.axis_size(axis)
    return lax.ppermute(array, axis, [(i, i + step) for i in range(size) if 0 <= i + step < size])


def local(estimate, views_data, psf_rows, psf_cols):
    views, planes, rows, _ = views_data.shape
    reach = (psf_rows.shape[1] - 1) // 2
    dims = (views, planes, rows, reach)
    tiles = planes * 2 * reach // LANES
    strip = (tiles + views) * rows
    vmem, hbm = pl.BlockSpec(memory_space=pltpu.VMEM), pl.BlockSpec(memory_space=pltpu.HBM)

    def call(kernel, in_specs, outs, scratch=(), room=16):
        return pl.pallas_call(
            functools.partial(kernel, dims),
            out_shape=outs,
            in_specs=in_specs,
            out_specs=jax.tree.map(lambda _: vmem, outs),
            scratch_shapes=scratch,
            compiler_params=pltpu.CompilerParams(vmem_limit_bytes=room << 20),
            cost_estimate=pl.CostEstimate(flops=1 << 20, bytes_accessed=1 << 20, transcendentals=0),
        )

    message = jax.ShapeDtypeStruct((strip, LANES), BF16)
    low, high = call(
        pack_kernel,
        [hbm] * 2,
        (message, message),
        [pltpu.VMEM(estimate.shape, F32), pltpu.VMEM(views_data.shape, BF16), pltpu.SemaphoreType.DMA((2,))],
    )(*(pltpu.with_memory_space_constraint(a, pltpu.HBM) for a in (estimate, views_data)))
    right = shift(low, "col", -1)
    left = shift(high, "col", 1)

    tall = rows + 2 * reach
    bands = call(
        bands_kernel,
        [vmem] * 2,
        (
            jax.ShapeDtypeStruct((views * tall, WIDE), BF16),
            jax.ShapeDtypeStruct((views, WIDE, WIDE), BF16),
            jax.ShapeDtypeStruct((views, WIDE, LANES), BF16),
            jax.ShapeDtypeStruct((views * rows, WIDE), BF16),
        ),
        [pltpu.VMEM((2, 8, LANES), F32)],
    )(psf_rows, psf_cols)

    length = planes * rows + views * planes * reach + 2 * (tiles * rows + views * reach)
    message = jax.ShapeDtypeStruct((length, LANES), BF16)
    bottom, top = call(rows_kernel, [vmem] * 4, (message, message))(estimate, views_data, right, left)
    above = shift(bottom, "row", 1)
    below = shift(top, "row", -1)
    return call(step_kernel, [vmem] * 10, jax.ShapeDtypeStruct(estimate.shape, F32))(
        estimate, views_data, right, left, above, below, *bands
    )


def solution(mesh):
    return jax.shard_map(
        local,
        mesh=mesh,
        in_specs=(P(None, "row", "col"), P(None, None, "row", "col"), P(), P()),
        out_specs=P(None, "row", "col"),
        check_vma=False,
    )
```

```python
import functools

import jax
import jax.numpy as jnp
from jax import lax
from jax.experimental import pallas as pl
from jax.experimental.pallas import tpu as pltpu
from jax.sharding import PartitionSpec as P

F32, BF16 = jnp.float32, jnp.bfloat16
LANES = 128
WIDE = 2 * LANES


def iota(shape, dim):
    return lax.broadcasted_iota(jnp.int32, shape, dim)


def pack_kernel(dims, est_hbm, views_hbm, low_ref, high_ref, est_ref, views_ref, sems):
    views, planes, rows, reach = dims
    wide, group = 2 * reach, LANES // (2 * reach)
    lane = iota((rows, LANES), 1)
    copies = [
        pltpu.make_async_copy(hbm, ref, sems.at[i])
        for i, (hbm, ref) in enumerate(((est_hbm, est_ref), (views_hbm, views_ref)))
    ]
    for copy in copies:
        copy.start()

    def strips(at, load, width, count):
        low = high = jnp.zeros((rows, LANES), F32)
        for k in range(count):
            block = pltpu.roll(load(k), k * width, 1) if k else load(k)
            low = jnp.where(lane // width == k, block, low)
            high = jnp.where(lane // width == (k - 1) % count, block, high)
        low_ref[at : at + rows, :] = low.astype(BF16)
        high_ref[at : at + rows, :] = high.astype(BF16)

    copies[0].wait()
    for t in range(planes // group):
        strips(t * rows, lambda k: est_ref[t * group + k], wide, group)
    base = planes // group * rows
    copies[1].wait()
    for v in range(views):
        strips(base + v * rows, lambda k: views_ref[v, k].astype(F32), reach, planes)


def rows_kernel(dims, est_ref, views_ref, right_ref, left_ref, first_ref, second_ref):
    views, planes, rows, reach = dims
    strip = planes * 2 * reach // LANES * rows
    upward = swaps_rows(lax.axis_index("col")) & (lax.axis_index("row") % 2 == 0)
    at = 0

    def both(block):
        for ref in (first_ref, second_ref):
            ref[at : at + block.shape[0], :] = block
        return at + block.shape[0]

    def sides(ref, base):
        top, bottom = ref[base : base + reach, :], ref[base + rows - reach : base + rows, :]
        first_ref[at : at + reach, :] = jnp.where(upward, top, bottom)
        second_ref[at : at + reach, :] = jnp.where(upward, bottom, top)
        return at + reach

    for p in range(planes):
        at = both(est_ref[p].astype(BF16))
    for v in range(views):
        for p in range(planes):
            at = sides(views_ref.at[v, p], 0)
    for c in (left_ref, right_ref):
        at = both(c[0:strip, :])
    for c in (left_ref, right_ref):
        for v in range(views):
            at = sides(c, strip + v * rows)


def bands_kernel(dims, psf_y_ref, psf_x_ref, ky_ref, kx_ref, kxt_ref, kyt_ref, taps_ref):
    views, planes, rows, reach = dims
    taps = 2 * reach + 1
    tall, full = rows + 2 * reach, rows + 4 * reach
    taps_ref[...] = jnp.zeros(taps_ref.shape, F32)
    for i, ref in enumerate((psf_y_ref, psf_x_ref)):
        psf = ref[...]
        taps_ref[i, 0:views, 0:taps] = psf / jnp.sum(psf, axis=1, keepdims=True)

    def band(i, v, tap, valid):
        source = jnp.broadcast_to(taps_ref[i, v : v + 1, :], tap.shape)
        inside = valid & (tap >= 0) & (tap < taps)
        return jnp.take_along_axis(source, jnp.where(inside, tap, LANES - 1), axis=1)

    def halves(w):
        hi = w.astype(BF16)
        return hi, (w - hi.astype(F32)).astype(BF16)

    def column(j, width):
        x = jnp.where(j < LANES, j, jnp.where(j < LANES + width, j - LANES - width, j - width))
        return x, j < LANES + 2 * width

    for half in range(2):
        lanes = slice(half * LANES, (half + 1) * LANES)
        row, lane = iota((tall, LANES), 0), iota((tall, LANES), 1) + half * LANES
        for v in range(views):
            hi, lo = halves(band(0, v, lax.rem(lane, full) - row, lane < 2 * full))
            ky_ref[v * tall : (v + 1) * tall, lanes] = jnp.where(lane < full, hi.astype(F32), lo.astype(F32)).astype(BF16)
        row, lane = iota((rows, LANES), 0), iota((rows, LANES), 1) + half * LANES
        for v in range(views):
            hi, lo = halves(band(0, v, row - lax.rem(lane, tall) + 2 * reach, lane < 3 * tall))
            pick = (lane >= tall) & (lane < 2 * tall)
            kyt_ref[v * rows : (v + 1) * rows, lanes] = jnp.where(pick, lo.astype(F32), hi.astype(F32)).astype(BF16)
        shape = (WIDE, LANES)
        source, ok_source = column(iota(shape, 0), 2 * reach)
        target, ok_target = column(iota(shape, 1) + half * LANES, reach)
        tap, ok = source - target + reach, ok_source & ok_target
        for v in range(views):
            kx_ref[v, :, lanes] = band(1, v, tap, ok).astype(BF16)
    source, ok = column(iota(shape, 0), reach)
    tap = iota(shape, 1) - source + reach
    for v in range(views):
        kxt_ref[v] = band(1, v, tap, ok).astype(BF16)


def step_kernel(dims, est_ref, views_ref, right_ref, left_ref, first_ref, second_ref, ky_ref, kx_ref, kxt_ref, kyt_ref, out_ref):
    views, planes, rows, reach = dims
    wide, group = 2 * reach, LANES // (2 * reach)
    tall = rows + 2 * reach
    tiles = planes // group
    own = planes * rows
    at_views = own
    at_c = own + views * planes * reach
    at_cv = at_c + 2 * tiles * rows

    turned = swaps_rows(lax.axis_index("col")) & (lax.axis_index("row") % 2 == 1)

    def tower(at, n, own):
        first, second = first_ref[at : at + n, :], second_ref[at : at + n, :]
        above, below = jnp.where(turned, second, first), jnp.where(turned, first, second)
        return jnp.concatenate([above, own, below], axis=0)

    def mixed(left, right, width):
        left, right = left.astype(F32), right.astype(F32)
        even = iota(left.shape, 1) // width % 2 == 0
        return jnp.where(even, right, left), jnp.where(even, left, right)

    def beside(tiles, k, width):
        shift = (1 - k) * width % LANES
        return pltpu.roll(tiles[k % 2], shift, 1) if shift else tiles[k % 2]

    blocks, halo = [], []
    for t in range(tiles):
        own = slice(t * rows, (t + 1) * rows)
        left = tower(at_c + t * rows, rows, left_ref[own, :])
        right = tower(at_c + (tiles + t) * rows, rows, right_ref[own, :])
        halo.append(mixed(left, right, wide))
    for p in range(planes):
        blocks.append(tower(p * rows, rows, est_ref[p].astype(BF16)))
        blocks.append(beside(halo[p // group], p % group, wide).astype(BF16))
    field = jnp.concatenate(blocks, axis=1)
    field = jnp.concatenate([field, field, jnp.zeros((WIDE - 2 * field.shape[0], field.shape[1]), BF16)], axis=0)

    lane = iota((tall, LANES), 1)
    product = None
    every = [
        jnp.dot(ky_ref[...], field[:, p * WIDE : (p + 1) * WIDE], preferred_element_type=F32).astype(BF16)
        for p in range(planes)
    ]
    def blur(v):
        rowed = jnp.concatenate([every[p][v * tall : (v + 1) * tall, :] for p in range(planes)], axis=0)
        return jnp.dot(rowed, kx_ref[v], preferred_element_type=F32)

    def divide(v, blurred):
        own = slice((tiles + v) * rows, (tiles + v + 1) * rows)
        left = tower(at_cv + v * reach, reach, left_ref[own, :])
        right = tower(at_cv + (views + v) * reach, reach, right_ref[own, :])
        rims = mixed(left, right, reach)
        quotients = []
        for p in range(planes):
            data = tower(at_views + (v * planes + p) * reach, reach, views_ref[v, p]).astype(F32)
            here = blurred[p * tall : (p + 1) * tall, :]
            main = data / here[:, :LANES]
            rim = jnp.where(lane < wide, beside(rims, p, reach) / here[:, LANES:], 0.0)
            quotients.append(jnp.concatenate([main.astype(BF16), rim.astype(BF16)], axis=1))
        return jnp.concatenate(quotients, axis=0)

    def planes_along_lanes(a):
        return jnp.concatenate([a[p * tall : (p + 1) * tall, :] for p in range(planes)], axis=1)

    def blur_back(v, quotient):
        back = jnp.dot(quotient, kxt_ref[v], preferred_element_type=F32)
        hi = back.astype(BF16)
        lo = (back - hi.astype(F32)).astype(BF16)
        hi, lo = planes_along_lanes(hi), planes_along_lanes(lo)
        return jnp.concatenate([hi, hi, lo, jnp.zeros((WIDE - 3 * tall, planes * LANES), BF16)], axis=0)

    def correct(v, back):
        return jnp.dot(kyt_ref[v * rows : (v + 1) * rows, :], back, preferred_element_type=F32)

    blurred = [blur(v) for v in range(views)]
    quotient = [divide(v, b) for v, b in enumerate(blurred)]
    back = [blur_back(v, q) for v, q in enumerate(quotient)]
    product = functools.reduce(jnp.multiply, [correct(v, b) for v, b in enumerate(back)])
    factor = jnp.sqrt(jnp.sqrt(product))
    for p in range(planes):
        out_ref[p] = est_ref[p] * factor[:, p * LANES : (p + 1) * LANES]


def shift(array, axis, step):
    size = lax.axis_size(axis)
    return lax.ppermute(array, axis, [(i, i + step) for i in range(size) if 0 <= i + step < size])


def swaps_rows(col):
    return col < 2


def along_rows(array, step):
    rows, cols = lax.axis_size("row"), lax.axis_size("col")
    pairs = []
    for i in range(rows):
        for j in range(cols):
            move = step if not swaps_rows(j) or i % 2 == 1 else -step
            if 0 <= i + move < rows:
                pairs.append((i * cols + j, (i + move) * cols + j))
    return lax.ppermute(array, ("row", "col"), pairs)


def local(estimate, views_data, psf_rows, psf_cols):
    views, planes, rows, _ = views_data.shape
    reach = (psf_rows.shape[1] - 1) // 2
    dims = (views, planes, rows, reach)
    tiles = planes * 2 * reach // LANES
    strip = (tiles + views) * rows
    vmem, hbm = pl.BlockSpec(memory_space=pltpu.VMEM), pl.BlockSpec(memory_space=pltpu.HBM)

    def call(kernel, in_specs, outs, scratch=(), room=16):
        return pl.pallas_call(
            functools.partial(kernel, dims),
            out_shape=outs,
            in_specs=in_specs,
            out_specs=jax.tree.map(lambda _: vmem, outs),
            scratch_shapes=scratch,
            compiler_params=pltpu.CompilerParams(vmem_limit_bytes=room << 20),
            cost_estimate=pl.CostEstimate(flops=1 << 20, bytes_accessed=1 << 20, transcendentals=0),
        )

    message = jax.ShapeDtypeStruct((strip, LANES), BF16)
    low, high = call(
        pack_kernel,
        [hbm] * 2,
        (message, message),
        [pltpu.VMEM(estimate.shape, F32), pltpu.VMEM(views_data.shape, BF16), pltpu.SemaphoreType.DMA((2,))],
    )(*(pltpu.with_memory_space_constraint(a, pltpu.HBM) for a in (estimate, views_data)))
    right = shift(low, "col", -1)
    left = shift(high, "col", 1)

    tall = rows + 2 * reach
    bands = call(
        bands_kernel,
        [vmem] * 2,
        (
            jax.ShapeDtypeStruct((views * tall, WIDE), BF16),
            jax.ShapeDtypeStruct((views, WIDE, WIDE), BF16),
            jax.ShapeDtypeStruct((views, WIDE, LANES), BF16),
            jax.ShapeDtypeStruct((views * rows, WIDE), BF16),
        ),
        [pltpu.VMEM((2, 8, LANES), F32)],
    )(psf_rows, psf_cols)

    length = planes * rows + views * planes * reach + 2 * (tiles * rows + views * reach)
    message = jax.ShapeDtypeStruct((length, LANES), BF16)
    first, second = call(rows_kernel, [vmem] * 4, (message, message))(estimate, views_data, right, left)
    first = along_rows(first, 1)
    second = along_rows(second, -1)
    return call(step_kernel, [vmem] * 10, jax.ShapeDtypeStruct(estimate.shape, F32))(
        estimate, views_data, right, left, first, second, *bands
    )


def solution(mesh):
    return jax.shard_map(
        local,
        mesh=mesh,
        in_specs=(P(None, "row", "col"), P(None, None, "row", "col"), P(), P()),
        out_specs=P(None, "row", "col"),
        check_vma=False,
    )
```

```python
import functools

import jax
import jax.numpy as jnp
from jax import lax
from jax.experimental import pallas as pl
from jax.experimental.pallas import tpu as pltpu
from jax.sharding import PartitionSpec as P

F32, BF16 = jnp.float32, jnp.bfloat16
LANES = 128
WIDE = 2 * LANES


def iota(shape, dim):
    return lax.broadcasted_iota(jnp.int32, shape, dim)


def pack_kernel(dims, est_hbm, views_hbm, low_ref, high_ref, est_ref, views_ref, sems):
    views, planes, rows, reach = dims
    wide, group = 2 * reach, LANES // (2 * reach)
    lane = iota((rows, LANES), 1)
    copies = [
        pltpu.make_async_copy(hbm, ref, sems.at[i])
        for i, (hbm, ref) in enumerate(((est_hbm, est_ref), (views_hbm, views_ref)))
    ]
    for copy in copies:
        copy.start()

    def strips(at, load, width, count):
        low = high = jnp.zeros((rows, LANES), F32)
        for k in range(count):
            block = pltpu.roll(load(k), k * width, 1) if k else load(k)
            low = jnp.where(lane // width == k, block, low)
            high = jnp.where(lane // width == (k - 1) % count, block, high)
        low_ref[at : at + rows, :] = low.astype(BF16)
        high_ref[at : at + rows, :] = high.astype(BF16)

    copies[0].wait()
    for t in range(planes // group):
        strips(t * rows, lambda k: est_ref[t * group + k], wide, group)
    base = planes // group * rows
    copies[1].wait()
    for v in range(views):
        strips(base + v * rows, lambda k: views_ref[v, k].astype(F32), reach, planes)


def rows_kernel(dims, est_ref, views_ref, right_ref, left_ref, first_ref, second_ref):
    views, planes, rows, reach = dims
    strip = planes * 2 * reach // LANES * rows
    upward = swaps_rows(lax.axis_index("col")) & (lax.axis_index("row") % 2 == 0)
    at = 0

    def both(block):
        for ref in (first_ref, second_ref):
            ref[at : at + block.shape[0], :] = block
        return at + block.shape[0]

    def sides(ref, base):
        top, bottom = ref[base : base + reach, :], ref[base + rows - reach : base + rows, :]
        first_ref[at : at + reach, :] = jnp.where(upward, top, bottom)
        second_ref[at : at + reach, :] = jnp.where(upward, bottom, top)
        return at + reach

    for p in range(planes):
        at = both(est_ref[p].astype(BF16))
    for v in range(views):
        for p in range(planes):
            at = sides(views_ref.at[v, p], 0)
    for c in (left_ref, right_ref):
        at = both(c[0:strip, :])
    for c in (left_ref, right_ref):
        for v in range(views):
            at = sides(c, strip + v * rows)


def bands_kernel(dims, psf_y_ref, psf_x_ref, ky_ref, kx_ref, kxt_ref, kyt_ref, taps_ref):
    views, planes, rows, reach = dims
    taps = 2 * reach + 1
    tall, full = rows + 2 * reach, rows + 4 * reach
    taps_ref[...] = jnp.zeros(taps_ref.shape, F32)
    for i, ref in enumerate((psf_y_ref, psf_x_ref)):
        psf = ref[...]
        taps_ref[i, 0:views, 0:taps] = psf / jnp.sum(psf, axis=1, keepdims=True)

    def band(i, v, tap, valid):
        source = jnp.broadcast_to(taps_ref[i, v : v + 1, :], tap.shape)
        inside = valid & (tap >= 0) & (tap < taps)
        return jnp.take_along_axis(source, jnp.where(inside, tap, LANES - 1), axis=1)

    def halves(w):
        hi = w.astype(BF16)
        return hi, (w - hi.astype(F32)).astype(BF16)

    def column(j, width):
        x = jnp.where(j < LANES, j, jnp.where(j < LANES + width, j - LANES - width, j - width))
        return x, j < LANES + 2 * width

    for half in range(2):
        lanes = slice(half * LANES, (half + 1) * LANES)
        row, lane = iota((tall, LANES), 0), iota((tall, LANES), 1) + half * LANES
        for v in range(views):
            hi, lo = halves(band(0, v, lax.rem(lane, full) - row, lane < 2 * full))
            ky_ref[v * tall : (v + 1) * tall, lanes] = jnp.where(lane < full, hi.astype(F32), lo.astype(F32)).astype(BF16)
        row, lane = iota((rows, LANES), 0), iota((rows, LANES), 1) + half * LANES
        for v in range(views):
            hi, lo = halves(band(0, v, row - lax.rem(lane, tall) + 2 * reach, lane < 3 * tall))
            pick = (lane >= tall) & (lane < 2 * tall)
            kyt_ref[v * rows : (v + 1) * rows, lanes] = jnp.where(pick, lo.astype(F32), hi.astype(F32)).astype(BF16)
        shape = (WIDE, LANES)
        source, ok_source = column(iota(shape, 0), 2 * reach)
        target, ok_target = column(iota(shape, 1) + half * LANES, reach)
        tap, ok = source - target + reach, ok_source & ok_target
        for v in range(views):
            kx_ref[v, :, lanes] = band(1, v, tap, ok).astype(BF16)
    source, ok = column(iota(shape, 0), reach)
    tap = iota(shape, 1) - source + reach
    for v in range(views):
        kxt_ref[v] = band(1, v, tap, ok).astype(BF16)


def step_kernel(dims, est_ref, views_ref, right_ref, left_ref, first_ref, second_ref, *refs):
    turned = swaps_rows(lax.axis_index("col")) & (lax.axis_index("row") % 2 == 1)
    step = functools.partial(join, dims, est_ref, views_ref, right_ref, left_ref)
    pl.when(turned)(lambda: step(second_ref, first_ref, *refs))
    pl.when(jnp.logical_not(turned))(lambda: step(first_ref, second_ref, *refs))


def join(dims, est_ref, views_ref, right_ref, left_ref, above_ref, below_ref, ky_ref, kx_ref, kxt_ref, kyt_ref, out_ref, result_ref, sems):
    views, planes, rows, reach = dims
    wide, group = 2 * reach, LANES // (2 * reach)
    tall = rows + 2 * reach
    tiles = planes // group
    own = planes * rows
    at_views = own
    at_c = own + views * planes * reach
    at_cv = at_c + 2 * tiles * rows

    def tower(at, n, own):
        return jnp.concatenate([above_ref[at : at + n, :], own, below_ref[at : at + n, :]], axis=0)

    def mixed(left, right, width):
        left, right = left.astype(F32), right.astype(F32)
        even = iota(left.shape, 1) // width % 2 == 0
        return jnp.where(even, right, left), jnp.where(even, left, right)

    def beside(tiles, k, width):
        shift = (1 - k) * width % LANES
        return pltpu.roll(tiles[k % 2], shift, 1) if shift else tiles[k % 2]

    blocks, halo = [], []
    for t in range(tiles):
        own = slice(t * rows, (t + 1) * rows)
        left = tower(at_c + t * rows, rows, left_ref[own, :])
        right = tower(at_c + (tiles + t) * rows, rows, right_ref[own, :])
        halo.append(mixed(left, right, wide))
    for p in range(planes):
        blocks.append(tower(p * rows, rows, est_ref[p].astype(BF16)))
        blocks.append(beside(halo[p // group], p % group, wide).astype(BF16))
    field = jnp.concatenate(blocks, axis=1)
    field = jnp.concatenate([field, field, jnp.zeros((WIDE - 2 * field.shape[0], field.shape[1]), BF16)], axis=0)

    lane = iota((tall, LANES), 1)
    product = None
    every = [
        jnp.dot(ky_ref[...], field[:, p * WIDE : (p + 1) * WIDE], preferred_element_type=F32).astype(BF16)
        for p in range(planes)
    ]
    def blur(v):
        rowed = jnp.concatenate([every[p][v * tall : (v + 1) * tall, :] for p in range(planes)], axis=0)
        return jnp.dot(rowed, kx_ref[v], preferred_element_type=F32)

    def divide(v, blurred):
        own = slice((tiles + v) * rows, (tiles + v + 1) * rows)
        left = tower(at_cv + v * reach, reach, left_ref[own, :])
        right = tower(at_cv + (views + v) * reach, reach, right_ref[own, :])
        rims = mixed(left, right, reach)
        quotients = []
        for p in range(planes):
            data = tower(at_views + (v * planes + p) * reach, reach, views_ref[v, p]).astype(F32)
            here = blurred[p * tall : (p + 1) * tall, :]
            main = data / here[:, :LANES]
            rim = jnp.where(lane < wide, beside(rims, p, reach) / here[:, LANES:], 0.0)
            quotients.append(jnp.concatenate([main.astype(BF16), rim.astype(BF16)], axis=1))
        return jnp.concatenate(quotients, axis=0)

    def planes_along_lanes(a):
        return jnp.concatenate([a[p * tall : (p + 1) * tall, :] for p in range(planes)], axis=1)

    def blur_back(v, quotient):
        back = jnp.dot(quotient, kxt_ref[v], preferred_element_type=F32)
        hi = back.astype(BF16)
        lo = (back - hi.astype(F32)).astype(BF16)
        hi, lo = planes_along_lanes(hi), planes_along_lanes(lo)
        return jnp.concatenate([hi, hi, lo, jnp.zeros((WIDE - 3 * tall, planes * LANES), BF16)], axis=0)

    def correct(v, back):
        return jnp.dot(kyt_ref[v * rows : (v + 1) * rows, :], back, preferred_element_type=F32)

    blurred = [blur(v) for v in range(views)]
    quotient = [divide(v, b) for v, b in enumerate(blurred)]
    back = [blur_back(v, q) for v, q in enumerate(quotient)]
    copies, part = [], planes // 2
    for start in range(0, planes, part):
        lanes = slice(start * LANES, (start + part) * LANES)
        product = functools.reduce(jnp.multiply, [correct(v, b[:, lanes]) for v, b in enumerate(back)])
        factor = jnp.sqrt(jnp.sqrt(product))
        for p in range(part):
            result_ref[start + p] = est_ref[start + p] * factor[:, p * LANES : (p + 1) * LANES]
        planes_done = pl.ds(start, part)
        copies.append(pltpu.make_async_copy(result_ref.at[planes_done], out_ref.at[planes_done], sems.at[len(copies)]))
        copies[-1].start()
    for copy in copies:
        copy.wait()


def shift(array, axis, step):
    size = lax.axis_size(axis)
    return lax.ppermute(array, axis, [(i, i + step) for i in range(size) if 0 <= i + step < size])


def swaps_rows(col):
    return col < 2


def along_rows(array, step):
    rows, cols = lax.axis_size("row"), lax.axis_size("col")
    pairs = []
    for i in range(rows):
        for j in range(cols):
            move = step if not swaps_rows(j) or i % 2 == 1 else -step
            if 0 <= i + move < rows:
                pairs.append((i * cols + j, (i + move) * cols + j))
    return lax.ppermute(array, ("row", "col"), pairs)


def local(estimate, views_data, psf_rows, psf_cols):
    views, planes, rows, _ = views_data.shape
    reach = (psf_rows.shape[1] - 1) // 2
    dims = (views, planes, rows, reach)
    tiles = planes * 2 * reach // LANES
    strip = (tiles + views) * rows
    vmem, hbm = pl.BlockSpec(memory_space=pltpu.VMEM), pl.BlockSpec(memory_space=pltpu.HBM)

    def call(kernel, in_specs, outs, scratch=(), room=16, out=None):
        return pl.pallas_call(
            functools.partial(kernel, dims),
            out_shape=outs,
            in_specs=in_specs,
            out_specs=jax.tree.map(lambda _: out or vmem, outs),
            scratch_shapes=scratch,
            compiler_params=pltpu.CompilerParams(vmem_limit_bytes=room << 20),
            cost_estimate=pl.CostEstimate(flops=1 << 20, bytes_accessed=1 << 20, transcendentals=0),
        )

    message = jax.ShapeDtypeStruct((strip, LANES), BF16)
    low, high = call(
        pack_kernel,
        [hbm] * 2,
        (message, message),
        [pltpu.VMEM(estimate.shape, F32), pltpu.VMEM(views_data.shape, BF16), pltpu.SemaphoreType.DMA((2,))],
    )(*(pltpu.with_memory_space_constraint(a, pltpu.HBM) for a in (estimate, views_data)))
    right = shift(low, "col", -1)
    left = shift(high, "col", 1)

    tall = rows + 2 * reach
    bands = call(
        bands_kernel,
        [vmem] * 2,
        (
            jax.ShapeDtypeStruct((views * tall, WIDE), BF16),
            jax.ShapeDtypeStruct((views, WIDE, WIDE), BF16),
            jax.ShapeDtypeStruct((views, WIDE, LANES), BF16),
            jax.ShapeDtypeStruct((views * rows, WIDE), BF16),
        ),
        [pltpu.VMEM((2, 8, LANES), F32)],
    )(psf_rows, psf_cols)

    length = planes * rows + views * planes * reach + 2 * (tiles * rows + views * reach)
    message = jax.ShapeDtypeStruct((length, LANES), BF16)
    first, second = call(rows_kernel, [vmem] * 4, (message, message))(estimate, views_data, right, left)
    first = along_rows(first, 1)
    second = along_rows(second, -1)
    return call(
        step_kernel,
        [vmem] * 10,
        jax.ShapeDtypeStruct(estimate.shape, F32),
        [pltpu.VMEM(estimate.shape, F32), pltpu.SemaphoreType.DMA((2,))],
        out=hbm,
    )(estimate, views_data, right, left, first, second, *bands)


def solution(mesh):
    return jax.shard_map(
        local,
        mesh=mesh,
        in_specs=(P(None, "row", "col"), P(None, None, "row", "col"), P(), P()),
        out_specs=P(None, "row", "col"),
        check_vma=False,
    )
```
